32 devices in a mesh: dp: 4 (over y, x), seq: 8 (over z, core).
Axes of the slice: x: 2, y: 2, z: 4, core: 2. Of those that a mesh axis runs over, the one named last changes fastest.
Arguments:
- inputs: bfloat16 [8, 1024, 1024], P('dp', 'seq'), may hold values from -6 to 6
- memory: bfloat16 [8, 512, 1024], P('dp', 'seq'), may hold values from -6 to 6
- mem_lengths: int32 [8], P('dp'), may hold values from 64 to 512, as said below
- cross_mask: int32 [8, 512], P('dp'), may hold values from 0 to 1, as said below
- buckets: int32 [1024], replicated, may hold values from 0 to 31
- self_query: bfloat16 [1024, 1024], P(('dp', 'seq')), may hold values from -0.1875 to 0.1875
- self_key: bfloat16 [1024, 512], P(('dp', 'seq')), may hold values from -0.1875 to 0.1875
- self_value: bfloat16 [1024, 512], P(('dp', 'seq')), may hold values from -0.1875 to 0.1875
- self_output: bfloat16 [1024, 1024], P(('dp', 'seq')), may hold values from -1.5 to 1.5
- cross_query: bfloat16 [1024, 1024], P(('dp', 'seq')), may hold values from -0.1875 to 0.1875
- cross_key: bfloat16 [1024, 512], P(('dp', 'seq')), may hold values from -0.1875 to 0.1875
- cross_value: bfloat16 [1024, 512], P(('dp', 'seq')), may hold values from -0.1875 to 0.1875
- cross_output: bfloat16 [1024, 1024], P(('dp', 'seq')), may hold values from -1 to 1
- gate_weight: bfloat16 [1024, 2816], P(('dp', 'seq')), may hold values from -0.1875 to 0.1875
- up_weight: bfloat16 [1024, 2816], P(('dp', 'seq')), may hold values from -0.1875 to 0.1875
- down_weight: bfloat16 [2816, 1024], P(('dp', 'seq')), may hold values from -0.15625 to 0.15625
- self_gain: bfloat16 [1024], P(('dp', 'seq')), may hold values from 0.5 to 1.5
- cross_gain: bfloat16 [1024], P(('dp', 'seq')), may hold values from 0.5 to 1.5
- feed_gain: bfloat16 [1024], P(('dp', 'seq')), may hold values from 0.5 to 1.5
- position_bias: bfloat16 [512], P(('dp', 'seq')), may hold values from -4 to 4
- cotangent: bfloat16 [8, 1024, 1024], P('dp', 'seq'), may hold values from -6 to 6
Outputs:
- output: bfloat16 [8, 1024, 1024], P('dp', 'seq')
- input_grad: float32 [8, 1024, 1024], P('dp', 'seq')
- memory_grad: float32 [8, 512, 1024], P('dp', 'seq')
- self_query_grad: float32 [1024, 1024], P(('dp', 'seq'))
- self_key_grad: float32 [1024, 512], P(('dp', 'seq'))
- self_value_grad: float32 [1024, 512], P(('dp', 'seq'))
- self_output_grad: float32 [1024, 1024], P(('dp', 'seq'))
- cross_query_grad: float32 [1024, 1024], P(('dp', 'seq'))
- cross_key_grad: float32 [1024, 512], P(('dp', 'seq'))
- cross_value_grad: float32 [1024, 512], P(('dp', 'seq'))
- cross_output_grad: float32 [1024, 1024], P(('dp', 'seq'))
- gate_weight_grad: float32 [1024, 2816], P(('dp', 'seq'))
- up_weight_grad: float32 [1024, 2816], P(('dp', 'seq'))
- down_weight_grad: float32 [2816, 1024], P(('dp', 'seq'))
- self_gain_grad: float32 [1024], P(('dp', 'seq'))
- cross_gain_grad: float32 [1024], P(('dp', 'seq'))
- feed_gain_grad: float32 [1024], P(('dp', 'seq'))
- position_bias_grad: float32 [512], P(('dp', 'seq'))
The draws below stay inside these ranges and needn't reach their ends.
Inputs may be any that keep to these rules, and one draw needn't show every extreme that they name: mem_lengths[s] counts the leading memory rows of sequence s that exist; one sequence has exactly 512 rows and one exactly 64. cross_mask[s, 0] is 1 for every sequence.
All inputs are finite; a program needn't handle non-finite values.
Results may differ from the reference program's by a relative error of at most 0.025.
Values may be sent and summed in bfloat16 or wider, within the bound.
No kernel may reach another device: no remote copies, remote signals or barrier semaphores. Data moves between devices by JAX's collectives and lax.ppermute only.
A program may use at most 192 MiB of HBM per device.

```python
import jax
import jax.numpy as jnp
from jax import lax

D = 1024
H = 16
HD = 64
FF = 2816
NB = 32
G = 8
LEN = 1024
MEM = 512
SEQS = 8


def draw_mem_lengths(key, part):
    counts = jax.random.randint(jax.random.fold_in(key, 11), (SEQS,), MEM // 8, MEM + 1)
    shuffled = jax.random.permutation(jax.random.fold_in(key, 12), SEQS)
    counts = counts.at[shuffled[0]].set(MEM).at[shuffled[1]].set(MEM // 8)
    return counts.astype(jnp.int32)


def draw_cross_mask(key, part):
    levels = jax.random.randint(jax.random.fold_in(key, 13), (SEQS, MEM), 0, 4)
    allowed = (levels > 0).astype(jnp.int32)
    return allowed.at[:, 0].set(1)


def place_ends(entries, own_key, low, largest):
    longest = entries.shape.index(max(entries.shape))
    spots = []
    for shift in (0, 1):
        where = [jax.random.randint(jax.random.fold_in(own_key, axis), (), 0, length) for axis, length in enumerate(entries.shape)]
        where[longest] = (where[longest] + shift) % entries.shape[longest]
        spots.append(tuple(where))
    return entries.at[spots[0]].set(low).at[spots[1]].set(largest)


def block_scale(key, extent, pieces, smallest, high):
    def one(axis_at, shards_of):
        draws = jax.random.uniform(jax.random.fold_in(jax.random.fold_in(key, 6), axis_at), (shards_of,), jnp.float32, smallest / len(pieces), high / len(pieces))
        return jnp.repeat(jnp.exp(draws), extent[axis_at] // shards_of).reshape((-1,) + (1,) * (len(extent) - axis_at - 1))

    level = one(*pieces[0])
    for cut in pieces[1:]:
        level = level * one(*cut)
    return level


def noise(rng, dims, spread, most, shards=(), kind=jnp.bfloat16):
    level = block_scale(rng, dims, shards, -0.22, 0.18) if shards else 1.0
    drawn = jax.random.normal(rng, dims, jnp.float32) * spread * level
    return jnp.minimum(jnp.maximum(drawn, -most), most).astype(kind)


def setup_inputs(seed: int = 0) -> dict:
    key_list = jax.random.split(jax.random.key(seed), 22)
    return {
        "inputs": noise(key_list[0], (SEQS, LEN, D), 1.0, 6.0, ((0, 4), (1, 8))),
        "memory": noise(key_list[1], (SEQS, MEM, D), 1.0, 6.0, ((0, 4), (1, 8))),
        "mem_lengths": draw_mem_lengths(jax.random.fold_in(key_list[21], 71), 0),
        "cross_mask": draw_cross_mask(jax.random.fold_in(key_list[21], 71), 0),
        "buckets": place_ends(jax.random.randint(key_list[4], (LEN,), 0, NB), jax.random.fold_in(key_list[4], 1), 0, NB - 1).astype(jnp.int32),
        "self_query": noise(key_list[5], (D, H * HD), D ** -0.5, 0.1875, ((0, 32),)),
        "self_key": noise(key_list[6], (D, G * HD), D ** -0.5, 0.1875, ((0, 32),)),
        "self_value": noise(key_list[7], (D, G * HD), D ** -0.5, 0.1875, ((0, 32),)),
        "self_output": noise(key_list[8], (H * HD, D), (H * HD // 64) ** -0.5, 1.5, ((0, 32),)),
        "cross_query": noise(key_list[9], (D, H * HD), D ** -0.5, 0.1875, ((0, 32),)),
        "cross_key": noise(key_list[10], (D, G * HD), D ** -0.5, 0.1875, ((0, 32),)),
        "cross_value": noise(key_list[11], (D, G * HD), D ** -0.5, 0.1875, ((0, 32),)),
        "cross_output": noise(key_list[12], (H * HD, D), (H * HD // 32) ** -0.5, 1.0, ((0, 32),)),
        "gate_weight": noise(key_list[13], (D, FF), D ** -0.5, 0.1875, ((0, 32),)),
        "up_weight": noise(key_list[14], (D, FF), D ** -0.5, 0.1875, ((0, 32),)),
        "down_weight": noise(key_list[15], (FF, D), (FF // 2) ** -0.5, 0.15625, ((0, 32),)),
        "self_gain": jnp.clip(1.0 + 0.1 * jax.random.normal(key_list[16], (D,), jnp.float32), 0.5, 1.5).astype(jnp.bfloat16),
        "cross_gain": jnp.clip(1.0 + 0.1 * jax.random.normal(key_list[17], (D,), jnp.float32), 0.5, 1.5).astype(jnp.bfloat16),
        "feed_gain": jnp.clip(1.0 + 0.1 * jax.random.normal(key_list[18], (D,), jnp.float32), 0.5, 1.5).astype(jnp.bfloat16),
        "position_bias": noise(key_list[19], (NB * H,), 1.0, 4.0, ((0, 32),)),
        "cotangent": noise(key_list[20], (SEQS, LEN, D), 1.0, 6.0, ((0, 4), (1, 8))),
    }


epsilon = 1e-06
highest = lax.Precision.HIGHEST
masked_out = -1e+30

@jax.custom_vjp
def low(v):
    return lax.optimization_barrier(v.astype(jnp.bfloat16)).astype(jnp.float32)

@jax.custom_vjp
def low_back(v):
    return v

def low_keep(v):
    return (low(v), None)

def low_pass(kept, grad):
    return (grad,)

def back_keep(v):
    return (v, None)

def back_low(kept, grad):
    return (low(grad),)
low.defvjp(low_keep, low_pass)
low_back.defvjp(back_keep, back_low)

def product(left, right):
    return jnp.dot(left, right, precision=highest)

def rms_scale(stream, norm_gain):
    return stream * lax.rsqrt(lax.optimization_barrier(jnp.mean(stream * stream, axis=-1, keepdims=True)) + epsilon) * norm_gain

def attention(queries, key_rows, value_rows, position_terms, allowed):
    query_count = queries.shape[0]
    key_count = key_rows.shape[0]
    query_heads = queries.reshape(query_count, G, H // G, HD)
    key_heads = key_rows.reshape(key_count, G, HD)
    value_heads = value_rows.reshape(key_count, G, HD)
    scores = HD ** (-0.5) * jnp.einsum('qgrd,kgd->grqk', query_heads, key_heads, precision=highest)
    logits = jnp.where(allowed, low_back(scores) + position_terms, masked_out)
    attn_weights = low(jax.nn.softmax(logits, axis=-1))
    combined = jnp.einsum('grqk,kgd->qgrd', attn_weights, value_heads, precision=highest)
    return combined.reshape(query_count, H * HD)

def decoder_layer(stream, memory_rows, weights, bucket_index, usable):
    query_self, key_self, value_self, output_self, query_cross, key_cross, value_cross, output_cross, gate_full, lift_full, down_full, gain_first, gain_second, gain_third, bias_table = weights
    positions = jnp.arange(LEN, dtype=jnp.int32)
    causal = positions[:, None] >= positions[None, :]
    position_terms = jnp.transpose(bias_table.reshape(NB, H)[bucket_index], (2, 0, 1)).reshape(G, H // G, LEN, LEN)
    act_first = low(rms_scale(stream, gain_first))
    queries = low(low_back(product(act_first, query_self)))
    key_rows = low(low_back(product(act_first, key_self)))
    value_rows = low(low_back(product(act_first, value_self)))
    self_att = low(low_back(attention(queries, key_rows, value_rows, position_terms, causal)))
    stream_one = stream + low_back(product(self_att, output_self))
    act_second = low(rms_scale(stream_one, gain_second))
    cross_queries = low(low_back(product(act_second, query_cross)))
    cross_keys = low(low_back(product(memory_rows, key_cross)))
    cross_values = low(low_back(product(memory_rows, value_cross)))
    cross_att = low(low_back(attention(cross_queries, cross_keys, cross_values, 0.0, usable[None, :])))
    stream_two = stream_one + low_back(product(cross_att, output_cross))
    act_third = low(rms_scale(stream_two, gain_third))
    gate_value = low_back(product(act_third, gate_full))
    lift_value = low_back(product(act_third, lift_full))
    hidden = low(jax.nn.gelu(gate_value, approximate=True) * lift_value)
    return stream_two + low_back(product(hidden, down_full))

def reference(inputs, memory, mem_lengths, cross_mask, buckets, self_query, self_key, self_value, self_output, cross_query, cross_key, cross_value, cross_output, gate_weight, up_weight, down_weight, self_gain, cross_gain, feed_gain, position_bias, cotangent):
    weights = tuple((matrix.astype(jnp.float32) for matrix in (self_query, self_key, self_value, self_output, cross_query, cross_key, cross_value, cross_output, gate_weight, up_weight, down_weight, self_gain, cross_gain, feed_gain, position_bias)))
    positions = jnp.arange(LEN, dtype=jnp.int32)
    bucket_index = buckets[jnp.clip(positions[:, None] - positions[None, :], 0, LEN - 1)]
    mem_rows = jnp.arange(MEM, dtype=jnp.int32)

    def one_sequence(totals, element):
        stream, memory_rows, length_one, mask_row, grad_row = element
        usable = (mask_row > 0) & (mem_rows < length_one)

        def forward(stream_in, memory_in, weight_in):
            return decoder_layer(stream_in, memory_in, weight_in, bucket_index, usable)
        result, pullback = jax.vjp(forward, stream.astype(jnp.float32), memory_rows.astype(jnp.float32), weights)
        grad_stream, grad_memory, grad_weights = pullback(grad_row.astype(jnp.float32))
        totals = jax.tree.map(jnp.add, totals, grad_weights)
        return (totals, (result.astype(jnp.bfloat16), grad_stream, grad_memory))
    start = tuple((jnp.zeros(matrix.shape, jnp.float32) for matrix in weights))
    totals, (outputs, input_grads, memory_grads) = lax.scan(one_sequence, start, (inputs, memory, mem_lengths, cross_mask, cotangent))
    return (outputs, input_grads, memory_grads, totals[0], totals[1], totals[2], totals[3], totals[4], totals[5], totals[6], totals[7], totals[8], totals[9], totals[10], totals[11], totals[12], totals[13], totals[14])
```

```python
import functools

import jax
import jax.numpy as jnp
from jax import lax
from jax.experimental import pallas as pl
from jax.experimental.pallas import tpu as pltpu
from jax.sharding import PartitionSpec as P

H = 16
HD = 64
NB = 32
G = 8
PER = H // G

epsilon = 1e-06
highest = lax.Precision.HIGHEST
masked_out = -1e30
bf16 = jnp.bfloat16
f32 = jnp.float32
LANES = 128


def layout():
    dp, seq = lax.axis_size("dp"), lax.axis_size("seq")
    return {
        "y": ("dp", dp // 2, 2),
        "x": ("dp", 1, dp // 2),
        "z": ("seq", 2, seq // 2),
        "c": ("seq", 1, 2),
    }


def my_digit(digit):
    axis, stride, size = digit
    return (lax.axis_index(axis) // stride) % size


def hop(value, digit):
    axis, stride, size = digit
    pairs = []
    for source in range(lax.axis_size(axis)):
        mine = (source // stride) % size
        pairs.append((source, source + ((mine + 1) % size - mine) * stride))
    return lax.ppermute(value, axis, pairs)


def gather_digit(value, digit, at):
    size, mine = digit[2], my_digit(digit)
    if size == 1:
        return jnp.expand_dims(value, at)
    if size == 2:
        other = hop(value, digit)
        upper = mine == 1
        return jnp.stack(
            [jnp.where(upper, other, value), jnp.where(upper, value, other)], axis=at
        )
    held = [value]
    for _ in range(size - 1):
        held.append(hop(held[-1], digit))
    turned = jnp.stack(held[::-1] + held[::-1], axis=at)
    return lax.dynamic_slice_in_dim(turned, size - 1 - mine, size, axis=at)


def reduce_digit(value, digit, at, kind=bf16):
    size, mine = digit[2], my_digit(digit)

    def piece(back):
        return lax.dynamic_index_in_dim(
            value, (mine - 1 - back + 2 * size) % size, at, keepdims=False
        )

    if size == 1:
        return jnp.squeeze(value, at).astype(kind)
    total = piece(0)
    for step in range(1, size):
        total = hop(total, digit).astype(f32) + piece(step).astype(f32)
        total = total.astype(kind if step == size - 1 else value.dtype)
    return total


def gather_all(shard, x_first):
    d = layout()
    held = gather_digit(shard, d["z"], 0)
    if x_first:
        held = gather_digit(gather_digit(held, d["x"], 0), d["y"], 0)
    else:
        held = gather_digit(gather_digit(held, d["y"], 0), d["x"], 1)
    held = gather_digit(held, d["c"], 3)
    return held.reshape((-1,) + shard.shape)


def scatter_all(value, x_last):
    d = layout()
    held = value.reshape(tuple(d[k][2] for k in "yxzc") + value.shape[1:])
    held = reduce_digit(held, d["c"], 3)
    if x_last:
        held = reduce_digit(reduce_digit(held, d["y"], 0), d["x"], 0)
    else:
        held = reduce_digit(reduce_digit(held, d["x"], 1), d["y"], 0)
    return reduce_digit(held, d["z"], 0, f32)


def heads_of(block, group):
    low = PER * group * HD
    return jnp.concatenate([block[:, low : low + HD], block[:, low + HD : low + 2 * HD]], axis=0)


def nt(left, right):
    return lax.dot_general(left, right, (((1,), (1,)), ((), ())), preferred_element_type=f32)


def attention_forward_kernel(causal, pad, start_ref, q_ref, k_ref, v_ref, b_ref, o_ref, p_ref):
    span = q_ref.shape[1]
    keys = k_ref[...].reshape(-1, LANES)
    values = v_ref[...].reshape(-1, LANES)
    queries = q_ref[0]
    length = keys.shape[0]
    for group in range(2):
        key_rows = keys[:, group * HD : (group + 1) * HD]
        value_rows = values[:, group * HD : (group + 1) * HD]
        scores = nt(heads_of(queries, group), key_rows) * HD ** (-0.5)
        if causal:
            tiles = []
            for head in (2 * group, 2 * group + 1):
                base = jnp.broadcast_to(b_ref[0, head : head + 1, :], (span, b_ref.shape[2]))
                tiles.append(pltpu.roll(base, 0, 1, stride=1, stride_axis=0)[:, pad:])
            row = lax.broadcasted_iota(jnp.int32, (span, length), 0) + start_ref[0]
            ahead = lax.broadcasted_iota(jnp.int32, (span, length), 1) > row
            tiles = [jnp.where(ahead, masked_out, tile) for tile in tiles]
            scores = scores + jnp.concatenate(tiles, axis=0)
        else:
            scores = scores + b_ref[0]
        peak = jnp.max(scores, axis=1, keepdims=True)
        exps = jnp.exp(scores - peak)
        probs = (exps * (1.0 / jnp.sum(exps, axis=1, keepdims=True))).astype(bf16)
        mixed = jnp.dot(probs, value_rows, preferred_element_type=f32).astype(bf16)
        for half in range(2):
            head = 2 * group + half
            p_ref[0, head] = probs[half * span : (half + 1) * span]
            o_ref[0, :, head * HD : (head + 1) * HD] = mixed[half * span : (half + 1) * span]


def sum_diagonals(tile):
    rows, width = tile.shape
    while rows > 1:
        rows //= 2
        tile = tile[:rows] + pltpu.roll(tile[rows:], width - rows, 1)
    return tile


def attention_backward_kernel(causal, pad, q_ref, k_ref, v_ref, g_ref, p_ref, *outs):
    dq_ref, dk_ref, dv_ref = outs[:3]
    span = q_ref.shape[1]
    keys = k_ref[...].reshape(-1, LANES)
    values = v_ref[...].reshape(-1, LANES)
    queries, grads = q_ref[0], g_ref[0]
    length = keys.shape[0]
    scaling = HD ** (-0.5)
    down_k, down_v = [], []
    for group in range(2):
        key_rows = keys[:, group * HD : (group + 1) * HD]
        value_rows = values[:, group * HD : (group + 1) * HD]
        query_rows = heads_of(queries, group)
        grad_rows = heads_of(grads, group)
        low_probs = p_ref[0, 2 * group : 2 * group + 2].reshape(2 * span, length)
        probs = low_probs.astype(f32)
        grad_probs = nt(grad_rows, value_rows)
        mean = jnp.sum(probs * grad_probs, axis=1, keepdims=True)
        grad_logits = probs * (grad_probs - mean)
        low = grad_logits.astype(bf16)
        dq = (jnp.dot(low, key_rows, preferred_element_type=f32) * scaling).astype(bf16)
        for half in range(2):
            head = 2 * group + half
            dq_ref[0, :, head * HD : (head + 1) * HD] = dq[half * span : (half + 1) * span]
        flat_q = query_rows.astype(f32).T.astype(bf16)
        flat_g = grad_rows.astype(f32).T.astype(bf16)
        down_k.append(jnp.dot(flat_q, low, preferred_element_type=f32) * scaling)
        down_v.append(jnp.dot(flat_g, low_probs, preferred_element_type=f32))
        if causal:
            for half in range(2):
                head = 2 * group + half
                tile = grad_logits[half * span : (half + 1) * span]
                wide = jnp.concatenate([jnp.zeros((span, pad), f32), tile], axis=1)
                outs[3][0, head : head + 1, :] = sum_diagonals(wide)
    dk_ref[...] = jnp.concatenate(down_k, axis=0).T.astype(bf16).reshape(dk_ref.shape)
    dv_ref[...] = jnp.concatenate(down_v, axis=0).T.astype(bf16).reshape(dv_ref.shape)


def attention_specs(queries, kv, bias):
    seqs, span, width = queries.shape
    blocks, _, rows, _ = kv.shape
    steps = width // (4 * HD)
    q_spec = pl.BlockSpec((1, span, 4 * HD), lambda s, j, *_: (s, 0, j))
    k_spec = pl.BlockSpec((blocks, 1, rows, LANES), lambda s, j, *_: (0, s, 0, j))
    v_spec = pl.BlockSpec((blocks, 1, rows, LANES), lambda s, j, *_: (0, s, 0, steps + j))
    p_spec = pl.BlockSpec((1, 4, span, blocks * rows), lambda s, j, *_: (s, j, 0, 0))
    return (seqs, steps), q_spec, k_spec, v_spec, p_spec


def attention_forward(queries, kv, bias, start, causal, pad):
    seqs, span, width = queries.shape
    length = kv.shape[0] * kv.shape[2]
    grid, q_spec, k_spec, v_spec, p_spec = attention_specs(queries, kv, bias)
    if causal:
        b_spec = pl.BlockSpec((1,) + bias.shape[1:], lambda s, j, *_: (j, 0, 0))
    else:
        b_spec = pl.BlockSpec((1,) + bias.shape[1:], lambda s, j, *_: (s, 0, 0))
    ops = seqs * H * span * length
    return pl.pallas_call(
        functools.partial(attention_forward_kernel, causal, pad),
        out_shape=(
            jax.ShapeDtypeStruct(queries.shape, bf16),
            jax.ShapeDtypeStruct((seqs, H, span, length), bf16),
        ),
        grid_spec=pltpu.PrefetchScalarGridSpec(
            num_scalar_prefetch=1,
            grid=grid,
            in_specs=[q_spec, k_spec, v_spec, b_spec],
            out_specs=(q_spec, p_spec),
        ),
        compiler_params=pltpu.CompilerParams(vmem_limit_bytes=40 << 20),
        cost_estimate=pl.CostEstimate(
            flops=4 * ops * HD, bytes_accessed=2 * ops, transcendentals=ops
        ),
        name="attend_causal" if causal else "attend_memory",
    )(start, queries, kv, kv, bias)


def attention_backward(queries, kv, grads, probs, causal, pad):
    seqs, span, width = queries.shape
    length = kv.shape[0] * kv.shape[2]
    grid, q_spec, k_spec, v_spec, p_spec = attention_specs(queries, kv, None)
    kv_out = jax.ShapeDtypeStruct(kv.shape[:3] + (G * HD,), bf16)
    kv_out_spec = k_spec
    out_shape = [jax.ShapeDtypeStruct(queries.shape, bf16), kv_out, kv_out]
    out_specs = [q_spec, kv_out_spec, kv_out_spec]
    if causal:
        out_shape.append(jax.ShapeDtypeStruct((seqs * grid[1], 4, pad + length), f32))
        steps = grid[1]
        out_specs.append(
            pl.BlockSpec((1, 4, pad + length), lambda s, j: (s * steps + j, 0, 0))
        )
    ops = seqs * H * span * length
    return pl.pallas_call(
        functools.partial(attention_backward_kernel, causal, pad),
        out_shape=out_shape,
        grid=grid,
        in_specs=[q_spec, k_spec, v_spec, q_spec, p_spec],
        out_specs=out_specs,
        compiler_params=pltpu.CompilerParams(vmem_limit_bytes=48 << 20),
        cost_estimate=pl.CostEstimate(flops=8 * ops * HD, bytes_accessed=2 * ops, transcendentals=0),
        name="attend_causal_back" if causal else "attend_memory_back",
    )(queries, kv, kv, grads, probs)


def rms_scale(stream, norm_gain):
    return (
        stream * lax.rsqrt(jnp.mean(stream * stream, axis=-1, keepdims=True) + epsilon) * norm_gain
    )


def gated_unit(gate_value, lift_value):
    return jax.nn.gelu(gate_value, approximate=True) * lift_value


def project(left, right):
    return jnp.dot(left, right, preferred_element_type=f32)


def project_back(left, right):
    return nt(left, right)


def weight_grad(left, right):
    return lax.dot_general(left, right, (((0,), (0,)), ((), ())), preferred_element_type=f32)


def shards(
    inputs,
    memory,
    mem_lengths,
    cross_mask,
    buckets,
    self_query,
    self_key,
    self_value,
    self_output,
    cross_query,
    cross_key,
    cross_value,
    cross_output,
    gate_weight,
    up_weight,
    down_weight,
    self_gain,
    cross_gain,
    feed_gain,
    position_bias,
    cotangent,
):
    seqs, span, width = inputs.shape
    mem_span = memory.shape[1]
    seq_count = lax.axis_size("seq")
    devices = seq_count * lax.axis_size("dp")
    length = span * seq_count
    mem_total = mem_span * seq_count
    rows = self_query.shape[0]
    kv_width = G * HD
    tokens = seqs * span
    pad = -(-span // LANES) * LANES
    first_row = lax.axis_index("seq") * span

    small = jnp.concatenate([self_gain, cross_gain, feed_gain, position_bias])
    small_count = small.shape[0]
    small_rows = 8 * -(-small_count // (8 * width))
    small = jnp.pad(small, (0, small_rows * width - small_count)).reshape(small_rows, width)
    part_a = jnp.concatenate(
        [self_query, jnp.concatenate([self_key, self_value], axis=1), small], axis=0
    )
    part_b = jnp.concatenate(
        [
            self_output,
            jnp.concatenate([cross_key, cross_value], axis=1),
            cross_query,
            cross_output,
        ],
        axis=0,
    )
    full_a = gather_all(part_a, True)
    full_b = gather_all(part_b, False)
    gate_full = gather_all(gate_weight, True).reshape(width, -1)
    lift_full = gather_all(up_weight, False).reshape(width, -1)
    down_full = gather_all(down_weight, True).reshape(-1, width)

    def cut(full, at, count=rows):
        return full[:, at : at + count].reshape(devices * count, width)

    query_self, kv_self = cut(full_a, 0), cut(full_a, rows)
    small_full = full_a[:, 2 * rows :].reshape(devices, small_rows * width)[:, :small_count]
    output_self, kv_cross = cut(full_b, 0), cut(full_b, rows)
    query_cross, output_cross = cut(full_b, 2 * rows), cut(full_b, 3 * rows)
    part = self_gain.shape[0]
    gain_first = small_full[:, :part].reshape(-1).astype(f32)
    gain_second = small_full[:, part : 2 * part].reshape(-1).astype(f32)
    gain_third = small_full[:, 2 * part : 3 * part].reshape(-1).astype(f32)
    bias_table = small_full[:, 3 * part :].reshape(NB, H)

    turned = jnp.pad(buckets[::-1], (pad, length), constant_values=-1)
    turned = lax.dynamic_slice(turned, (length - 1 - first_row,), (pad + length,))
    one_hot = turned[None, :] == jnp.arange(NB, dtype=jnp.int32)[:, None]
    terms = jnp.einsum(
        "bh,bc->hc", bias_table, one_hot.astype(bf16), preferred_element_type=f32
    ).reshape(H // 4, 4, pad + length)
    start = jnp.reshape(first_row, (1,)).astype(jnp.int32)

    stream = inputs.reshape(tokens, width).astype(f32)
    mem_block = memory.reshape(seqs * mem_span, width)
    act_first = rms_scale(stream, gain_first).astype(bf16)
    local_kv = project(act_first, kv_self).astype(bf16).reshape(seqs, span, 2 * kv_width)
    full_kv = lax.all_gather(local_kv, "seq", axis=0)
    memory_kv = project(mem_block, kv_cross).astype(bf16).reshape(seqs, mem_span, 2 * kv_width)
    full_memory_kv = lax.all_gather(memory_kv, "seq", axis=0)
    queries = project(act_first, query_self).astype(bf16).reshape(seqs, span, H * HD)
    self_att, self_probs = attention_forward(queries, full_kv, terms, start, True, pad)
    flat_self = self_att.reshape(tokens, H * HD)
    stream_one = stream + project(flat_self, output_self)
    act_second = rms_scale(stream_one, gain_second).astype(bf16)
    cross_queries = project(act_second, query_cross).astype(bf16).reshape(seqs, span, H * HD)
    usable = (cross_mask > 0) & (
        jnp.arange(mem_total, dtype=jnp.int32)[None, :] < mem_lengths[:, None]
    )
    shut = jnp.where(usable, 0.0, masked_out).astype(f32)[:, None, :]
    cross_att, cross_probs = attention_forward(
        cross_queries, full_memory_kv, shut, start, False, pad
    )
    flat_cross = cross_att.reshape(tokens, H * HD)
    stream_two = stream_one + project(flat_cross, output_cross)
    act_third = rms_scale(stream_two, gain_third).astype(bf16)
    gate_value = project(act_third, gate_full)
    lift_value = project(act_third, lift_full)
    hidden = gated_unit(gate_value, lift_value).astype(bf16)
    output = (stream_two + project(hidden, down_full)).astype(bf16)

    low_down = cotangent.reshape(tokens, width)
    grad_stream = low_down.astype(f32)
    grad_down = weight_grad(hidden, low_down).astype(bf16)
    grad_hidden = project_back(low_down, down_full)
    grad_gate, grad_lift = jax.vjp(gated_unit, gate_value, lift_value)[1](grad_hidden)
    low_gate = grad_gate.astype(bf16)
    low_lift = grad_lift.astype(bf16)
    grad_gate_weight = weight_grad(act_third, low_gate).astype(bf16)
    grad_lift_weight = weight_grad(act_third, low_lift).astype(bf16)

    def by_device(grad):
        return grad.reshape(devices, -1, grad.shape[-1])

    down_total = scatter_all(by_device(grad_down), True)
    gate_total = scatter_all(by_device(grad_gate_weight), False)
    lift_total = scatter_all(by_device(grad_lift_weight), True)

    grad_act = project_back(low_gate, gate_full) + project_back(low_lift, lift_full)
    grad_norm, grad_gain_third = jax.vjp(rms_scale, stream_two, gain_third)[1](grad_act)
    grad_stream = grad_stream + grad_norm
    low_branch = grad_stream.astype(bf16)
    grad_output_cross = weight_grad(flat_cross, low_branch).astype(bf16)
    grad_cross_att = project_back(low_branch, output_cross).astype(bf16)
    grad_cq, grad_ck, grad_cv = attention_backward(
        cross_queries,
        full_memory_kv,
        grad_cross_att.reshape(seqs, span, H * HD),
        cross_probs,
        False,
        pad,
    )
    memory_kv_grad = lax.psum_scatter(
        jnp.concatenate([grad_ck, grad_cv], axis=-1), "seq", scatter_dimension=0
    ).reshape(seqs * mem_span, 2 * kv_width)
    grad_kv_cross = weight_grad(mem_block, memory_kv_grad).astype(bf16)
    memory_grad = project_back(memory_kv_grad, kv_cross)
    low_cq = grad_cq.reshape(tokens, H * HD)
    grad_query_cross = weight_grad(act_second, low_cq).astype(bf16)
    grad_act = project_back(low_cq, query_cross)
    grad_norm, grad_gain_second = jax.vjp(rms_scale, stream_one, gain_second)[1](grad_act)
    grad_stream = grad_stream + grad_norm
    low_branch = grad_stream.astype(bf16)
    grad_output_self = weight_grad(flat_self, low_branch).astype(bf16)
    total_b = scatter_all(
        jnp.concatenate(
            [
                by_device(g)
                for g in (grad_output_self, grad_kv_cross, grad_query_cross, grad_output_cross)
            ],
            axis=1,
        ),
        False,
    )
    grad_self_att = project_back(low_branch, output_self).astype(bf16)
    grad_sq, grad_sk, grad_sv, diagonals = attention_backward(
        queries, full_kv, grad_self_att.reshape(seqs, span, H * HD), self_probs, True, pad
    )
    grad_table = jnp.einsum(
        "hc,bc->bh",
        jnp.sum(diagonals.reshape(seqs, H, pad + length), axis=0),
        one_hot.astype(f32),
        precision=highest,
    )
    local_kv_grad = lax.psum_scatter(
        jnp.concatenate([grad_sk, grad_sv], axis=-1), "seq", scatter_dimension=0
    ).reshape(tokens, 2 * kv_width)
    low_sq = grad_sq.reshape(tokens, H * HD)
    grad_query_self = weight_grad(act_first, low_sq).astype(bf16)
    grad_kv_self = weight_grad(act_first, local_kv_grad).astype(bf16)
    grad_act = project_back(low_sq, query_self) + project_back(local_kv_grad, kv_self)
    grad_norm, grad_gain_first = jax.vjp(rms_scale, stream, gain_first)[1](grad_act)
    input_grad = grad_stream + grad_norm
    small_grad = jnp.concatenate(
        [
            grad_gain_first.reshape(devices, -1),
            grad_gain_second.reshape(devices, -1),
            grad_gain_third.reshape(devices, -1),
            grad_table.reshape(devices, -1),
        ],
        axis=1,
    )
    small_grad = jnp.pad(small_grad, ((0, 0), (0, small_rows * width - small_count)))
    total_a = scatter_all(
        jnp.concatenate(
            [
                by_device(grad_query_self),
                by_device(grad_kv_self),
                small_grad.astype(bf16).reshape(devices, small_rows, width),
            ],
            axis=1,
        ),
        True,
    )
    small_total = total_a[2 * rows :].reshape(-1)[:small_count]

    def row_block(total, index):
        return total[index * rows : (index + 1) * rows]

    kv_total, cross_kv_total = row_block(total_a, 1), row_block(total_b, 1)
    return (
        output.reshape(inputs.shape),
        input_grad.reshape(inputs.shape),
        memory_grad.reshape(memory.shape),
        row_block(total_a, 0),
        kv_total[:, :kv_width],
        kv_total[:, kv_width:],
        row_block(total_b, 0),
        row_block(total_b, 2),
        cross_kv_total[:, :kv_width],
        cross_kv_total[:, kv_width:],
        row_block(total_b, 3),
        gate_total,
        lift_total,
        down_total,
        small_total[:part],
        small_total[part : 2 * part],
        small_total[2 * part : 3 * part],
        small_total[3 * part :],
    )


def solution(mesh):
    rows_split = P("dp", "seq", None)
    weight_split = P(("dp", "seq"), None)
    vector_split = P(("dp", "seq"))
    return jax.shard_map(
        shards,
        mesh=mesh,
        in_specs=(rows_split, rows_split, P("dp"), P("dp", None), P())
        + (weight_split,) * 11
        + (vector_split,) * 4
        + (rows_split,),
        out_specs=(rows_split,) * 3 + (weight_split,) * 11 + (vector_split,) * 4,
        check_vma=False,
    )
```
